768 devices in a mesh: ctx: 64 (over y, x, core), head: 12 (over z).
Axes of the slice: x: 4, y: 8, z: 12, core: 2. Of those that a mesh axis runs over, the one named last changes fastest.
Arguments:
- query_heads: bfloat16 [16384, 48, 128], P('ctx', 'head'), may hold values from -5 to 5
- key_head: bfloat16 [16384, 6, 128], P('ctx'), may hold values from -5 to 5
- value_head: bfloat16 [16384, 6, 128], P('ctx'), may hold values from -5 to 5
- out_grad: bfloat16 [16384, 48, 128], P('ctx', 'head'), may hold values from -5 to 5
- doc_blocks: int32 [32], replicated, may hold values from 1 to 8, 128 in all
Outputs:
- query_grad: bfloat16 [16384, 48, 128], P('ctx', 'head')
- key_grad: bfloat16 [16384, 6, 128], P('ctx')
- value_grad: bfloat16 [16384, 6, 128], P('ctx')
The draws below stay inside these ranges and needn't reach their ends.
Inputs may be any that keep to these rules, and one draw needn't show every extreme that they name: `doc_blocks`: every document has 1 to 8 blocks, together 16384 // 128 blocks, and one document has exactly 8 blocks.
All inputs are finite; a program needn't handle non-finite values.
Results may differ from the reference program's by a relative error of at most 0.025.
Values may be sent and summed in bfloat16 or wider, within the bound.
A program may use at most 32 MiB of HBM per device.

```python
import math
import jax
import jax.numpy as jnp
import numpy as np
from jax import lax

HD = 128
GROUP = 8
BLOCK = 128
QHEADS = 48
KVH = 6
TOKENS = 16384
MAX_DOC = 1024
DOCS = 32


def draw_query_heads(key, part):
    base = jnp.clip(jax.random.normal(jax.random.fold_in(key, 11), (TOKENS, QHEADS, HD), jnp.float32), -4.0, 4.0)
    return base.astype(jnp.bfloat16)


def draw_key_head(key, part):
    base = jnp.clip(jax.random.normal(jax.random.fold_in(key, 13), (TOKENS, KVH, HD), jnp.float32), -4.0, 4.0)
    return base.astype(jnp.bfloat16)


def block_scale(own_key, shape, split, least, high):
    def one(axis_at, blocks):
        heights = jax.random.uniform(jax.random.fold_in(jax.random.fold_in(own_key, 6), axis_at), (blocks,), jnp.float32, least / len(split), high / len(split))
        return jnp.repeat(jnp.exp(heights), shape[axis_at] // blocks).reshape((-1,) + (1,) * (len(shape) - axis_at - 1))

    gain = one(*split[0])
    for cut in split[1:]:
        gain = gain * one(*cut)
    return gain


def profile(amount, total, reach, lean):
    loads = [(1 << 20) // math.isqrt(rank ** lean) + 1 for rank in range(2, amount + 1)]
    spare, counts = total - reach - (amount - 1), [1] * (amount - 1)
    while spare > 0:
        candidates = [i for i in range(amount - 1) if counts[i] < reach]
        pool, remaining = sum([loads[i] for i in candidates]), spare
        for i in candidates:
            extra = min(reach - counts[i], max(1, remaining * loads[i] // pool), spare)
            counts[i] = counts[i] + extra
            spare = spare - extra
    return np.array([reach] + counts)


def uneven(stream_key, number_of, total, most, slope):
    if number_of == 2:
        one = jax.random.randint(stream_key, (), max(1, total - most), min(most, total - 1) + 1)
        return jnp.stack([one, total - one])
    sizes = jnp.asarray(profile(number_of, total, most, slope), jnp.int32)
    couples = (number_of - 1) // 2
    donor, taker = sizes[1:1 + 2 * couples:2], sizes[2:2 + 2 * couples:2]
    room = jnp.minimum(donor - 1, most - taker)
    passed = jax.random.randint(jax.random.fold_in(stream_key, 1), (couples,), 0, 1 << 20) % (room + 1)
    sizes = sizes.at[1:1 + 2 * couples:2].set(donor - passed).at[2:2 + 2 * couples:2].set(taker + passed)
    return sizes[jax.random.permutation(jax.random.fold_in(stream_key, 2), number_of)]


def noise(own_key, extent, width, bound, cuts=(), held_as=jnp.bfloat16):
    values = jax.random.normal(own_key, extent, jnp.float32) * width
    if len(cuts) > 0:
        values = block_scale(own_key, extent, cuts, -0.22, 0.18) * values
    return jnp.clip(values, min=-bound, max=bound).astype(held_as)


def setup_inputs(seed: int = 0) -> dict:
    key_of = jax.random.split(jax.random.key(seed), 6)
    return {
        "query_heads": draw_query_heads(jax.random.fold_in(key_of[5], 71), 0),
        "key_head": draw_key_head(jax.random.fold_in(key_of[5], 71), 0),
        "value_head": noise(key_of[2], (TOKENS, KVH, HD), 1.0, 5.0, ((0, 64),)),
        "out_grad": noise(key_of[3], (TOKENS, QHEADS, HD), 1.0, 5.0, ((0, 64), (1, 12))),
        "doc_blocks": uneven(key_of[4], DOCS, TOKENS // BLOCK, MAX_DOC // BLOCK, 2).astype(jnp.int32),
    }


masked_value = -1e30


def doc_index(positions, doc_ends):
    return jnp.sum((positions[:, None] >= doc_ends[None, :]).astype(jnp.int32), axis=1).astype(jnp.int32)


def to_low(values):
    return lax.optimization_barrier(values.astype(jnp.bfloat16)).astype(jnp.float32)


def reference(query_heads, key_head, value_head, out_grad, doc_blocks):
    score_scale = HD ** -0.5
    doc_ends = (jnp.cumsum(doc_blocks) * BLOCK).astype(jnp.int32)
    positions = jnp.arange(TOKENS, dtype=jnp.int32)
    doc_of = doc_index(positions, doc_ends)
    margin = MAX_DOC - BLOCK
    key_pad = jnp.concatenate([jnp.zeros((margin, KVH, HD), key_head.dtype), key_head], axis=0)
    value_pad = jnp.concatenate([jnp.zeros((margin, KVH, HD), value_head.dtype), value_head], axis=0)
    doc_pad = jnp.concatenate([jnp.full((margin,), -1, jnp.int32), doc_of], axis=0)

    def one_block(carry, block_index):
        key_acc, value_acc = carry
        start = (block_index * BLOCK).astype(jnp.int32)
        zero = jnp.zeros((), jnp.int32)
        query_blk = lax.dynamic_slice(query_heads, (start, zero, zero), (BLOCK, QHEADS, HD)).astype(jnp.float32).reshape(BLOCK, KVH, GROUP, HD)
        grad_blk = lax.dynamic_slice(out_grad, (start, zero, zero), (BLOCK, QHEADS, HD)).astype(jnp.float32).reshape(BLOCK, KVH, GROUP, HD)
        key_blk = lax.dynamic_slice(key_pad, (start, zero, zero), (MAX_DOC, KVH, HD)).astype(jnp.float32)
        value_blk = lax.dynamic_slice(value_pad, (start, zero, zero), (MAX_DOC, KVH, HD)).astype(jnp.float32)
        key_docs = lax.dynamic_slice(doc_pad, (start,), (MAX_DOC,))
        query_docs = lax.dynamic_slice(doc_of, (start,), (BLOCK,))
        query_pos = start + jnp.arange(BLOCK, dtype=jnp.int32)
        key_pos = start - margin + jnp.arange(MAX_DOC, dtype=jnp.int32)
        allowed = (query_docs[:, None] == key_docs[None, :]) & (key_pos[None, :] <= query_pos[:, None])
        scores = jnp.einsum('ikgd,jkd->kgij', query_blk, key_blk) * score_scale
        scores = jnp.where(allowed[None, None], scores, masked_value)
        row_max = jnp.max(scores, axis=3, keepdims=True)
        row_sum = jnp.sum(jnp.exp(scores - row_max), axis=3, keepdims=True)
        log_norm = row_max + jnp.log(row_sum)
        probs = jnp.exp(scores - log_norm)
        probs_low = to_low(probs)
        attended = to_low(jnp.einsum('kgij,jkd->ikgd', probs_low, value_blk))
        out_dot = jnp.transpose(jnp.sum(grad_blk * attended, axis=3), (1, 2, 0))
        dprob = jnp.einsum('ikgd,jkd->kgij', grad_blk, value_blk)
        dscore = to_low(probs * (dprob - out_dot[:, :, :, None]))
        query_part = jnp.einsum('kgij,jkd->ikgd', dscore, key_blk) * score_scale
        key_part = jnp.einsum('kgij,ikgd->jkd', dscore, query_blk)
        value_part = jnp.einsum('kgij,ikgd->jkd', probs_low, grad_blk)
        key_acc = lax.dynamic_update_slice(key_acc, lax.dynamic_slice(key_acc, (start, zero, zero), (MAX_DOC, KVH, HD)) + key_part, (start, zero, zero))
        value_acc = lax.dynamic_update_slice(value_acc, lax.dynamic_slice(value_acc, (start, zero, zero), (MAX_DOC, KVH, HD)) + value_part, (start, zero, zero))
        return (key_acc, value_acc), query_part.reshape(BLOCK, QHEADS, HD).astype(jnp.bfloat16)

    zero_acc = jnp.zeros((TOKENS + margin, KVH, HD), jnp.float32)
    (key_acc, value_acc), query_parts = lax.scan(one_block, (zero_acc, zero_acc), jnp.arange(TOKENS // BLOCK, dtype=jnp.int32))
    query_grad = query_parts.reshape(TOKENS, QHEADS, HD)
    key_grad = (key_acc[margin:] * score_scale).astype(jnp.bfloat16)
    value_grad = value_acc[margin:].astype(jnp.bfloat16)
    return (query_grad, key_grad, value_grad)
```

```python
import functools

import jax
import jax.numpy as jnp
from jax import lax
from jax.experimental import pallas as pl
from jax.experimental.pallas import tpu as pltpu
from jax.sharding import PartitionSpec as P

GROUP = 8
BLOCK = 128
REACH = 8
MASKED = -1e30
LOG2E = 1.4426950408889634
MESH = pl.DeviceIdType.MESH
CHUNKS = 4

NT = (((1,), (1,)), ((), ()))
NN = (((1,), (0,)), ((), ()))
TN = (((0,), (0,)), ((), ()))


def dot(a, b, dims):
    return lax.dot_general(a, b, dims, preferred_element_type=jnp.float32)


def kernel(
    n_ctx, n_head, heads, docs,
    docs_ref, q_hbm, do_hbm, k_hbm, v_hbm,
    dq_out, kv_out,
    q_ref, do_ref, kw, vw, e_ref, dp_ref, stat, ds_ref, own, sb, rb, og, dq_ref,
    load_sem, a_send, a_recv, b_send, b_recv, c_send, c_recv, out_sem,
):
    width = q_ref.shape[1]
    shard = 2 * BLOCK
    rows = BLOCK * heads
    scale = width ** -0.5
    to_log2 = scale * LOG2E
    s = lax.axis_index("ctx")
    h = lax.axis_index("head")
    role = lax.rem(h, 2)
    partner = h + 1 - 2 * role
    other = lax.rem(h - 1 + 2 * role + n_head, n_head)
    up = lax.rem(h + 1, n_head)
    down = lax.rem(h + n_head - 1, n_head)
    group = h * heads // GROUP

    def ctx(delta):
        return lax.rem(s + delta + n_ctx, n_ctx)

    loads = [
        pltpu.make_async_copy(k_hbm.at[group], kw.at[pl.ds(7 * BLOCK, shard)], load_sem.at[0]),
        pltpu.make_async_copy(v_hbm.at[group], vw.at[pl.ds(7 * BLOCK, shard)], load_sem.at[1]),
        pltpu.make_async_copy(q_hbm, q_ref, load_sem.at[2]),
        pltpu.make_async_copy(do_hbm, do_ref, load_sem.at[3]),
    ]
    for copy in loads:
        copy.start()

    barrier = pltpu.get_barrier_semaphore()
    peers = [(ctx(d), h) for d in range(-4, 5) if d != 0]
    peers += [(ctx(d), partner) for d in range(-4, 5)] + [(s, other)]
    for peer in peers:
        pl.semaphore_signal(barrier, inc=1, device_id=peer, device_id_type=MESH)
    pl.semaphore_wait(barrier, len(peers))

    sends = []
    fetch = {}
    for d in (4, 3, 2, 1):
        size, first = (shard, 0) if d < 4 else (BLOCK, BLOCK)
        at = (7 - 2 * d) * BLOCK + first
        for i, (src, dst) in enumerate(((k_hbm, kw), (v_hbm, vw))):
            copy = pltpu.make_async_remote_copy(
                src_ref=src.at[group, pl.ds(first, size)],
                dst_ref=dst.at[pl.ds(at, size)],
                send_sem=a_send.at[d - 1, i],
                recv_sem=a_recv.at[d - 1, i],
                device_id=(ctx(d), h),
                device_id_type=MESH,
            )
            copy.start()
            sends.append(copy)
            fetch[d, i] = copy

    before = []
    for qb in range(2):
        at = 2 * s + qb
        total = jnp.int32(0)
        start = jnp.int32(0)
        for i in range(docs):
            start = jnp.where(total <= at, total, start)
            total = total + docs_ref[i]
        before.append(at - start)

    for copy in loads:
        copy.wait()

    key_at = lax.broadcasted_iota(jnp.int32, (BLOCK, rows), 0)
    query_at = lax.broadcasted_iota(jnp.int32, (BLOCK, rows), 1) // heads
    causal = key_at <= query_at

    def pair(qb, w):
        back = 7 + qb - w
        q = q_ref[pl.ds(qb * rows, rows), :]
        do = do_ref[pl.ds(qb * rows, rows), :]
        scores = dot(kw[pl.ds(w * BLOCK, BLOCK), :], q, NT)
        if back == 0:
            scores = jnp.where(causal, scores, MASKED)
        top = jnp.max(scores, axis=0, keepdims=True) * to_log2
        e = jnp.exp2(scores * to_log2 - top)
        dp = dot(vw[pl.ds(w * BLOCK, BLOCK), :], do, NT)
        at = w - qb
        e_ref[qb, pl.ds(at * BLOCK, BLOCK), :] = e
        dp_ref[qb, pl.ds(at * BLOCK, BLOCK), :] = dp
        bias = jnp.where(back <= before[qb], jnp.float32(0), jnp.float32(MASKED))
        stat[qb, 0, pl.ds(at, 1), :] = top + bias
        stat[qb, 1, pl.ds(at, 1), :] = jnp.sum(e, axis=0, keepdims=True)
        stat[qb, 2, pl.ds(at, 1), :] = jnp.sum(e * dp, axis=0, keepdims=True)

    pair(0, 7)
    pair(1, 7)
    pair(1, 8)
    for d in (1, 2, 3, 4):
        fetch[d, 0].wait_recv()
        fetch[d, 1].wait_recv()
        if d < 4:
            for w in (7 - 2 * d, 8 - 2 * d):
                pair(0, w)
                pair(1, w)
        else:
            pair(0, 0)

    factors, dots = [], []
    for qb in range(2):
        tops = stat[qb, 0]
        part = jnp.exp2(tops - jnp.max(tops, axis=0, keepdims=True))
        inv = 1.0 / jnp.sum(stat[qb, 1] * part, axis=0, keepdims=True)
        factors.append(part * inv)
        dots.append(jnp.sum(stat[qb, 2] * part, axis=0, keepdims=True) * inv)

    back_sends = []
    back_recv = {}

    def key_block(w):
        grads = [None, None]
        for qb in range(2):
            at = w - qb
            if not 0 <= at < REACH:
                continue
            probs = e_ref[qb, pl.ds(at * BLOCK, BLOCK), :] * factors[qb][at : at + 1]
            dscore = (probs * (dp_ref[qb, pl.ds(at * BLOCK, BLOCK), :] - dots[qb])).astype(jnp.bfloat16)
            ds_ref[qb, pl.ds(at * BLOCK, BLOCK), :] = dscore
            terms = (
                dot(dscore, q_ref[pl.ds(qb * rows, rows), :], NN),
                dot(probs.astype(jnp.bfloat16), do_ref[pl.ds(qb * rows, rows), :], NN),
            )
            grads = [t if g is None else g + t for g, t in zip(grads, terms)]
        grads[0] = grads[0] * scale
        d, half = (8 - w) // 2, (w + 1) % 2
        for i in range(2):
            sb[w, i] = grads[i].astype(jnp.bfloat16)
            if d == 0:
                own[i, pl.ds(half * BLOCK, BLOCK), :] = grads[i]
        for plane, row in enumerate((h, partner)):
            if d == 0 and plane == 0:
                continue
            which = role if plane == 0 else 1 - role
            copy = pltpu.make_async_remote_copy(
                src_ref=sb.at[w, which],
                dst_ref=rb.at[plane, d, pl.ds(half * BLOCK, BLOCK)],
                send_sem=b_send.at[plane, d, half],
                recv_sem=b_recv.at[plane, d, half],
                device_id=(ctx(-d), row),
                device_id_type=MESH,
            )
            copy.start()
            back_sends.append(copy)
            back_recv[plane, d, half] = copy

    for w in (1, 3, 5, 7, 0, 2, 4, 6, 8):
        key_block(w)

    for qb in range(2):
        grad = dot(kw[pl.ds(qb * BLOCK, REACH * BLOCK), :], ds_ref[qb], TN)
        dq_ref[pl.ds(qb * rows, rows), :] = (jnp.transpose(grad) * scale).astype(jnp.bfloat16)
    dq_copy = pltpu.make_async_copy(dq_ref, dq_out, out_sem.at[n_head])
    dq_copy.start()

    piece = shard // CHUNKS
    far = n_head // 2

    def hop(step, chunk, way):
        origin = lax.rem(h + n_head - step, n_head) if way == 0 else lax.rem(h + step, n_head)
        part = og.at[origin, pl.ds(chunk * piece, piece)]
        return pltpu.make_async_remote_copy(
            src_ref=part,
            dst_ref=part,
            send_sem=c_send.at[way, step, chunk],
            recv_sem=c_recv.at[way, step, chunk],
            device_id=(s, up if way == 0 else down),
            device_id_type=MESH,
        )

    def hops(chunk, way):
        return far if (chunk % 2 == 0) == (way == 0) else n_head - 1 - far

    ring = {}
    for half in range(2):
        total = own[role, pl.ds(half * BLOCK, BLOCK), :]
        for (plane, d, at), copy in back_recv.items():
            if at == half:
                copy.wait_recv()
                total = total + rb[plane, d, pl.ds(half * BLOCK, BLOCK), :].astype(jnp.float32)
        og[h, pl.ds(half * BLOCK, BLOCK), :] = total.astype(jnp.bfloat16)
        for chunk in range(half * CHUNKS // 2, (half + 1) * CHUNKS // 2):
            for way in range(2):
                ring[0, chunk, way] = hop(0, chunk, way)
                ring[0, chunk, way].start()

    outs = []

    def put(origin, index):
        copy = pltpu.make_async_copy(og.at[origin], kv_out.at[lax.rem(origin, 2), origin // 2], out_sem.at[index])
        copy.start()
        outs.append(copy)

    put(h, 0)
    for step in range(1, far + 1):
        for chunk in range(CHUNKS):
            for way in range(2):
                if step <= hops(chunk, way):
                    ring[step - 1, chunk, way].wait_recv()
                if step < hops(chunk, way):
                    ring[step, chunk, way] = hop(step, chunk, way)
                    ring[step, chunk, way].start()
        put(lax.rem(h + n_head - step, n_head), 2 * step - 1)
        if step < far:
            put(lax.rem(h + step, n_head), 2 * step)

    for copy in sends + back_sends + list(ring.values()):
        copy.wait_send()
    dq_copy.wait()
    for copy in outs:
        copy.wait()


def on_device(query_heads, key_head, value_head, out_grad, doc_blocks, n_ctx, n_head):
    tokens, heads, width = query_heads.shape
    kv_count = key_head.shape[1]
    rows = BLOCK * heads
    flat = lambda x: x.reshape(tokens * heads, width)
    dma = pltpu.SemaphoreType.DMA
    bf16, f32 = jnp.bfloat16, jnp.float32
    window = (REACH + 1) * BLOCK
    dq, kv = pl.pallas_call(
        functools.partial(kernel, n_ctx, n_head, heads, doc_blocks.shape[0]),
        out_shape=(
            jax.ShapeDtypeStruct((tokens * heads, width), bf16),
            jax.ShapeDtypeStruct((2, kv_count, tokens, width), bf16),
        ),
        in_specs=[pl.BlockSpec(memory_space=pltpu.SMEM)] + [pl.BlockSpec(memory_space=pl.ANY)] * 4,
        out_specs=(pl.BlockSpec(memory_space=pl.ANY),) * 2,
        scratch_shapes=[
            pltpu.VMEM((tokens * heads, width), bf16),
            pltpu.VMEM((tokens * heads, width), bf16),
            pltpu.VMEM((window, width), bf16),
            pltpu.VMEM((window, width), bf16),
            pltpu.VMEM((2, REACH * BLOCK, rows), f32),
            pltpu.VMEM((2, REACH * BLOCK, rows), f32),
            pltpu.VMEM((2, 3, REACH, rows), f32),
            pltpu.VMEM((2, REACH * BLOCK, rows), bf16),
            pltpu.VMEM((2, 2 * BLOCK, width), f32),
            pltpu.VMEM((REACH + 1, 2, BLOCK, width), bf16),
            pltpu.VMEM((2, 5, 2 * BLOCK, width), bf16),
            pltpu.VMEM((n_head, tokens, width), bf16),
            pltpu.VMEM((tokens * heads, width), bf16),
            dma((4,)),
            dma((4, 2)),
            dma((4, 2)),
            dma((2, 5, 2)),
            dma((2, 5, 2)),
            dma((2, n_head // 2, CHUNKS)),
            dma((2, n_head // 2, CHUNKS)),
            dma((n_head + 1,)),
        ],
        compiler_params=pltpu.CompilerParams(
            collective_id=0, has_side_effects=True, vmem_limit_bytes=48 * 1024 * 1024
        ),
        name="attention_backward",
    )(
        doc_blocks,
        flat(query_heads),
        flat(out_grad),
        jnp.transpose(key_head, (1, 0, 2)),
        jnp.transpose(value_head, (1, 0, 2)),
    )
    kv = jnp.transpose(kv, (0, 2, 1, 3))
    return dq.reshape(tokens, heads, width), kv[0], kv[1]


def solution(mesh):
    return jax.shard_map(
        functools.partial(on_device, n_ctx=mesh.shape["ctx"], n_head=mesh.shape["head"]),
        mesh=mesh,
        in_specs=(
            P("ctx", "head", None),
            P("ctx", None, None),
            P("ctx", None, None),
            P("ctx", "head", None),
            P(),
        ),
        out_specs=(P("ctx", "head", None), P("ctx", None, None), P("ctx", None, None)),
        check_vma=False,
    )
```

```python
import functools

import jax
import jax.numpy as jnp
from jax import lax
from jax.experimental import pallas as pl
from jax.experimental.pallas import tpu as pltpu
from jax.sharding import PartitionSpec as P

GROUP = 8
BLOCK = 128
REACH = 8
MASKED = -1e30
LOG2E = 1.4426950408889634
MESH = pl.DeviceIdType.MESH
CHUNKS = 4

NT = (((1,), (1,)), ((), ()))
NN = (((1,), (0,)), ((), ()))
TN = (((0,), (0,)), ((), ()))


def dot(a, b, dims):
    return lax.dot_general(a, b, dims, preferred_element_type=jnp.float32)


def kernel(
    n_ctx, n_head, heads, docs,
    docs_ref, q_hbm, do_hbm, k_hbm, v_hbm,
    dq_out, kv_out,
    q_ref, do_ref, kw, vw, e_ref, dp_ref, stat, ds_ref, own, sb, rb, og, dq_ref,
    load_sem, a_send, a_recv, b_send, b_recv, c_send, c_recv, out_sem,
):
    width = q_ref.shape[1]
    shard = 2 * BLOCK
    rows = BLOCK * heads
    scale = width ** -0.5
    to_log2 = scale * LOG2E
    s = lax.axis_index("ctx")
    h = lax.axis_index("head")
    role = lax.rem(h, 2)
    partner = h + 1 - 2 * role
    other = lax.rem(h - 1 + 2 * role + n_head, n_head)
    up = lax.rem(h + 1, n_head)
    down = lax.rem(h + n_head - 1, n_head)
    group = h * heads // GROUP

    core = lax.rem(s, 2)
    sibling = s + 1 - 2 * core

    def ctx(delta):
        return lax.rem(s + delta + n_ctx, n_ctx)

    def slot(d, first=0, size=shard):
        return pl.ds((8 - 2 * d) * BLOCK + first, size)

    loads = [
        pltpu.make_async_copy(k_hbm.at[group], kw.at[slot(0)], load_sem.at[0]),
        pltpu.make_async_copy(v_hbm.at[group], vw.at[slot(0)], load_sem.at[1]),
        pltpu.make_async_copy(q_hbm, q_ref, load_sem.at[2]),
        pltpu.make_async_copy(do_hbm, do_ref, load_sem.at[3]),
    ]
    for copy in loads:
        copy.start()

    barrier = pltpu.get_barrier_semaphore()
    peers = [(ctx(d), h) for d in range(-4, 5) if d != 0]
    peers += [(ctx(d), partner) for d in range(-4, 5)] + [(s, other)]
    for peer in peers:
        pl.semaphore_signal(barrier, inc=1, device_id=peer, device_id_type=MESH)
    pl.semaphore_wait(barrier, len(peers))

    pairs = ((k_hbm, kw), (v_hbm, vw))

    def push(i, src, dst, sem, target):
        return pltpu.make_async_remote_copy(
            src_ref=src,
            dst_ref=dst,
            send_sem=a_send.at[sem, i],
            recv_sem=a_recv.at[sem, i],
            device_id=(target, h),
            device_id_type=MESH,
        )

    def far_half(i, half):
        src, dst = pairs[i]
        at = half * BLOCK
        return push(i, src.at[group, pl.ds(at, BLOCK)], dst.at[slot(4, at, BLOCK)], half, ctx(4))

    def near(i):
        src, dst = pairs[i]
        return push(i, src.at[group], dst.at[slot(2)], 2, ctx(2))

    def across_near(i):
        dst = pairs[i][1]
        to = pl.ds((2 + 4 * core) * BLOCK, shard)
        return push(i, dst.at[slot(2)], dst.at[to], 3, sibling)

    def across_own(i):
        src, dst = pairs[i]
        return push(i, src.at[group], dst.at[slot(1)], 4, sibling)

    def across_far(i):
        dst = pairs[i][1]
        return push(i, dst.at[slot(4)], dst.at[slot(3)], 4, sibling)

    for i in range(2):
        far_half(i, 1).start()

    @pl.when(core == 1)
    def _():
        for i in range(2):
            far_half(i, 0).start()

    for i in range(2):
        near(i).start()

    @pl.when(core == 0)
    def _():
        for i in range(2):
            across_own(i).start()

    before = []
    for qb in range(2):
        at = 2 * s + qb
        total = jnp.int32(0)
        start = jnp.int32(0)
        for i in range(docs):
            start = jnp.where(total <= at, total, start)
            total = total + docs_ref[i]
        before.append(at - start)

    for copy in loads:
        copy.wait()

    key_at = lax.broadcasted_iota(jnp.int32, (BLOCK, rows), 0)
    query_at = lax.broadcasted_iota(jnp.int32, (BLOCK, rows), 1) // heads
    causal = key_at <= query_at

    def pair(qb, w):
        back = 7 + qb - w
        q = q_ref[pl.ds(qb * rows, rows), :]
        do = do_ref[pl.ds(qb * rows, rows), :]
        scores = dot(kw[pl.ds((w + 1) * BLOCK, BLOCK), :], q, NT)
        if back == 0:
            scores = jnp.where(causal, scores, MASKED)
        top = jnp.max(scores, axis=0, keepdims=True) * to_log2
        e = jnp.exp2(scores * to_log2 - top)
        dp = dot(vw[pl.ds((w + 1) * BLOCK, BLOCK), :], do, NT)
        at = w - qb
        e_ref[qb, pl.ds(at * BLOCK, BLOCK), :] = e
        dp_ref[qb, pl.ds(at * BLOCK, BLOCK), :] = dp
        bias = jnp.where(back <= before[qb], jnp.float32(0), jnp.float32(MASKED))
        stat[qb, 0, pl.ds(at, 1), :] = top + bias
        stat[qb, 1, pl.ds(at, 1), :] = jnp.sum(e, axis=0, keepdims=True)
        stat[qb, 2, pl.ds(at, 1), :] = jnp.sum(e * dp, axis=0, keepdims=True)

    pair(0, 7)
    pair(1, 7)
    pair(1, 8)
    for i in range(2):
        far_half(i, 1).wait_recv()

    @pl.when(core == 1)
    def _():
        for i in range(2):
            far_half(i, 0).wait_recv()
            across_far(i).start()

    for i in range(2):
        near(i).wait_recv()
        across_near(i).start()
    pair(0, 0)
    for w in (3, 4):
        pair(0, w)
        pair(1, w)
    for i in range(2):
        across_far(i).wait_recv()
        across_near(i).wait_recv()
    for w in (1, 2, 5, 6):
        pair(0, w)
        pair(1, w)

    factors, dots = [], []
    for qb in range(2):
        tops = stat[qb, 0]
        part = jnp.exp2(tops - jnp.max(tops, axis=0, keepdims=True))
        inv = 1.0 / jnp.sum(stat[qb, 1] * part, axis=0, keepdims=True)
        factors.append(part * inv)
        dots.append(jnp.sum(stat[qb, 2] * part, axis=0, keepdims=True) * inv)

    back_sends = []
    back_recv = {}

    def key_block(w):
        grads = [None, None]
        for qb in range(2):
            at = w - qb
            if not 0 <= at < REACH:
                continue
            probs = e_ref[qb, pl.ds(at * BLOCK, BLOCK), :] * factors[qb][at : at + 1]
            dscore = (probs * (dp_ref[qb, pl.ds(at * BLOCK, BLOCK), :] - dots[qb])).astype(jnp.bfloat16)
            ds_ref[qb, pl.ds(at * BLOCK, BLOCK), :] = dscore
            terms = (
                dot(dscore, q_ref[pl.ds(qb * rows, rows), :], NN),
                dot(probs.astype(jnp.bfloat16), do_ref[pl.ds(qb * rows, rows), :], NN),
            )
            grads = [t if g is None else g + t for g, t in zip(grads, terms)]
        grads[0] = grads[0] * scale
        d, half = (8 - w) // 2, (w + 1) % 2
        for i in range(2):
            sb[w, i] = grads[i].astype(jnp.bfloat16)
            if d == 0:
                own[i, pl.ds(half * BLOCK, BLOCK), :] = grads[i]
        for plane, row in enumerate((h, partner)):
            if d == 0 and plane == 0:
                continue
            which = role if plane == 0 else 1 - role
            copy = pltpu.make_async_remote_copy(
                src_ref=sb.at[w, which],
                dst_ref=rb.at[plane, d, pl.ds(half * BLOCK, BLOCK)],
                send_sem=b_send.at[plane, d, half],
                recv_sem=b_recv.at[plane, d, half],
                device_id=(ctx(-d), row),
                device_id_type=MESH,
            )
            copy.start()
            back_sends.append(copy)
            back_recv[plane, d, half] = copy

    for w in (1, 3, 5, 7, 0, 2, 4, 6, 8):
        key_block(w)

    for qb in range(2):
        grad = dot(kw[pl.ds((qb + 1) * BLOCK, REACH * BLOCK), :], ds_ref[qb], TN)
        dq_ref[pl.ds(qb * rows, rows), :] = (jnp.transpose(grad) * scale).astype(jnp.bfloat16)
    dq_copy = pltpu.make_async_copy(dq_ref, dq_out, out_sem.at[n_head])
    dq_copy.start()

    piece = shard // CHUNKS
    far = n_head // 2

    def hop(step, chunk, way):
        origin = lax.rem(h + n_head - step, n_head) if way == 0 else lax.rem(h + step, n_head)
        part = og.at[origin, pl.ds(chunk * piece, piece)]
        return pltpu.make_async_remote_copy(
            src_ref=part,
            dst_ref=part,
            send_sem=c_send.at[way, step, chunk],
            recv_sem=c_recv.at[way, step, chunk],
            device_id=(s, up if way == 0 else down),
            device_id_type=MESH,
        )

    def hops(chunk, way):
        return far if (chunk % 2 == 0) == (way == 0) else n_head - 1 - far

    for half in range(2):
        total = own[role, pl.ds(half * BLOCK, BLOCK), :]
        for (plane, d, at), copy in back_recv.items():
            if at == half:
                copy.wait_recv()
                total = total + rb[plane, d, pl.ds(half * BLOCK, BLOCK), :].astype(jnp.float32)
        og[h, pl.ds(half * BLOCK, BLOCK), :] = total.astype(jnp.bfloat16)
        for chunk in range(half * CHUNKS // 2, (half + 1) * CHUNKS // 2):
            for way in range(2):
                hop(0, chunk, way).start()

    outs = []

    def put(origin, index):
        copy = pltpu.make_async_copy(og.at[origin], kv_out.at[lax.rem(origin, 2), origin // 2], out_sem.at[index])
        copy.start()
        outs.append(copy)

    put(h, 0)

    def advance(step, way):
        for chunk in range(CHUNKS):
            if step <= hops(chunk, way):
                hop(step - 1, chunk, way).wait_recv()
            if step < hops(chunk, way):
                hop(step, chunk, way).start()

    for step in range(1, far + 1):
        pl.when(step <= h)(functools.partial(advance, step, 0))
    for step in range(1, far + 1):
        advance(step, 1)
        if step < far:
            put(lax.rem(h + step, n_head), 2 * step)
    for step in range(1, far + 1):
        pl.when(step > h)(functools.partial(advance, step, 0))
    for step in range(1, far + 1):
        put(lax.rem(h + n_head - step, n_head), 2 * step - 1)

    for copy in back_sends:
        copy.wait_send()
    for i in range(2):
        far_half(i, 1).wait_send()
        near(i).wait_send()
        across_near(i).wait_send()
        across_own(i).wait_send()

    @pl.when(core == 1)
    def _():
        for i in range(2):
            far_half(i, 0).wait_send()

    for way in range(2):
        for chunk in range(CHUNKS):
            for step in range(hops(chunk, way)):
                hop(step, chunk, way).wait_send()
    dq_copy.wait()
    for copy in outs:
        copy.wait()


def on_device(query_heads, key_head, value_head, out_grad, doc_blocks, n_ctx, n_head):
    tokens, heads, width = query_heads.shape
    kv_count = key_head.shape[1]
    rows = BLOCK * heads
    flat = lambda x: x.reshape(tokens * heads, width)
    dma = pltpu.SemaphoreType.DMA
    bf16, f32 = jnp.bfloat16, jnp.float32
    window = (REACH + 2) * BLOCK
    dq, kv = pl.pallas_call(
        functools.partial(kernel, n_ctx, n_head, heads, doc_blocks.shape[0]),
        out_shape=(
            jax.ShapeDtypeStruct((tokens * heads, width), bf16),
            jax.ShapeDtypeStruct((2, kv_count, tokens, width), bf16),
        ),
        in_specs=[pl.BlockSpec(memory_space=pltpu.SMEM)] + [pl.BlockSpec(memory_space=pl.ANY)] * 4,
        out_specs=(pl.BlockSpec(memory_space=pl.ANY),) * 2,
        scratch_shapes=[
            pltpu.VMEM((tokens * heads, width), bf16),
            pltpu.VMEM((tokens * heads, width), bf16),
            pltpu.VMEM((window, width), bf16),
            pltpu.VMEM((window, width), bf16),
            pltpu.VMEM((2, REACH * BLOCK, rows), f32),
            pltpu.VMEM((2, REACH * BLOCK, rows), f32),
            pltpu.VMEM((2, 3, REACH, rows), f32),
            pltpu.VMEM((2, REACH * BLOCK, rows), bf16),
            pltpu.VMEM((2, 2 * BLOCK, width), f32),
            pltpu.VMEM((REACH + 1, 2, BLOCK, width), bf16),
            pltpu.VMEM((2, 5, 2 * BLOCK, width), bf16),
            pltpu.VMEM((n_head, tokens, width), bf16),
            pltpu.VMEM((tokens * heads, width), bf16),
            dma((4,)),
            dma((5, 2)),
            dma((5, 2)),
            dma((2, 5, 2)),
            dma((2, 5, 2)),
            dma((2, n_head // 2, CHUNKS)),
            dma((2, n_head // 2, CHUNKS)),
            dma((n_head + 1,)),
        ],
        compiler_params=pltpu.CompilerParams(
            collective_id=0, has_side_effects=True, vmem_limit_bytes=67043328
        ),
        name="attention_backward",
    )(
        doc_blocks,
        flat(query_heads),
        flat(out_grad),
        jnp.transpose(key_head, (1, 0, 2)),
        jnp.transpose(value_head, (1, 0, 2)),
    )
    kv = jnp.transpose(kv, (0, 2, 1, 3))
    return dq.reshape(tokens, heads, width), kv[0], kv[1]


def solution(mesh):
    return jax.shard_map(
        functools.partial(on_device, n_ctx=mesh.shape["ctx"], n_head=mesh.shape["head"]),
        mesh=mesh,
        in_specs=(
            P("ctx", "head", None),
            P("ctx", None, None),
            P("ctx", None, None),
            P("ctx", "head", None),
            P(),
        ),
        out_specs=(P("ctx", "head", None), P("ctx", None, None), P("ctx", None, None)),
        check_vma=False,
    )
```

```python
import functools

import jax
import jax.numpy as jnp
from jax import lax
from jax.experimental import pallas as pl
from jax.experimental.pallas import tpu as pltpu
from jax.sharding import PartitionSpec as P

GROUP = 8
BLOCK = 128
REACH = 8
MASKED = -1e30
LOG2E = 1.4426950408889634
MESH = pl.DeviceIdType.MESH
CHUNKS = 4

NT = (((1,), (1,)), ((), ()))
NN = (((1,), (0,)), ((), ()))
TN = (((0,), (0,)), ((), ()))


def dot(a, b, dims):
    return lax.dot_general(a, b, dims, preferred_element_type=jnp.float32)


def kernel(
    n_ctx, n_head, heads, docs,
    docs_hbm, q_hbm, do_hbm, k_hbm, v_hbm,
    dq_out, kv_out,
    docs_ref, q_ref, do_ref, kw, vw, e_ref, dp_ref, stat, ds_ref, own, sb, rb, og, dq_ref,
    load_sem, a_send, a_recv, b_send, b_recv, c_send, c_recv, out_sem,
):
    width = q_ref.shape[1]
    shard = 2 * BLOCK
    rows = BLOCK * heads
    scale = width ** -0.5
    to_log2 = scale * LOG2E
    s = lax.axis_index("ctx")
    h = lax.axis_index("head")
    role = lax.rem(h, 2)
    partner = h + 1 - 2 * role
    other = lax.rem(h - 1 + 2 * role + n_head, n_head)
    group = h * heads // GROUP

    core = lax.rem(s, 2)
    sibling = s + 1 - 2 * core

    def ctx(delta):
        return lax.rem(s + delta + n_ctx, n_ctx)

    def slot(d, first=0, size=shard):
        return pl.ds((8 - 2 * d) * BLOCK + first, size)

    loads = [
        pltpu.make_async_copy(k_hbm.at[group], kw.at[slot(0)], load_sem.at[0]),
        pltpu.make_async_copy(v_hbm.at[group], vw.at[slot(0)], load_sem.at[1]),
        pltpu.make_async_copy(q_hbm, q_ref, load_sem.at[2]),
        pltpu.make_async_copy(do_hbm, do_ref, load_sem.at[3]),
        pltpu.make_async_copy(docs_hbm, docs_ref, load_sem.at[4]),
    ]
    for copy in loads:
        copy.start()

    barrier = pltpu.get_barrier_semaphore()
    peers = [(ctx(d), h) for d in range(-4, 5) if d != 0]
    peers += [(ctx(d), partner) for d in range(-4, 5)] + [(s, other), (s, lax.rem(h + 2, n_head)), (s, lax.rem(h + n_head - 2, n_head))]
    for peer in peers:
        pl.semaphore_signal(barrier, inc=1, device_id=peer, device_id_type=MESH)
    pl.semaphore_wait(barrier, len(peers))

    pairs = ((k_hbm, kw), (v_hbm, vw))

    def push(i, src, dst, sem, target):
        return pltpu.make_async_remote_copy(
            src_ref=src,
            dst_ref=dst,
            send_sem=a_send.at[sem, i],
            recv_sem=a_recv.at[sem, i],
            device_id=(target, h),
            device_id_type=MESH,
        )

    def far_half(i, half):
        src, dst = pairs[i]
        at = half * BLOCK
        return push(i, src.at[group, pl.ds(at, BLOCK)], dst.at[slot(4, at, BLOCK)], half, ctx(4))

    def near(i):
        src, dst = pairs[i]
        return push(i, src.at[group], dst.at[slot(2)], 2, ctx(2))

    def across_near(i):
        dst = pairs[i][1]
        to = pl.ds((2 + 4 * core) * BLOCK, shard)
        return push(i, dst.at[slot(2)], dst.at[to], 3, sibling)

    def across_own(i):
        src, dst = pairs[i]
        return push(i, src.at[group], dst.at[slot(1)], 4, sibling)

    def across_far(i):
        dst = pairs[i][1]
        return push(i, dst.at[slot(4)], dst.at[slot(3)], 4, sibling)

    for i in range(2):
        far_half(i, 1).start()

    @pl.when(core == 1)
    def _():
        for i in range(2):
            far_half(i, 0).start()

    for i in range(2):
        near(i).start()

    @pl.when(core == 0)
    def _():
        for i in range(2):
            across_own(i).start()

    for copy in loads:
        copy.wait()

    before = []
    for qb in range(2):
        at = 2 * s + qb
        total = jnp.int32(0)
        start = jnp.int32(0)
        for i in range(docs):
            start = jnp.where(total <= at, total, start)
            total = total + docs_ref[i]
        before.append(at - start)

    key_at = lax.broadcasted_iota(jnp.int32, (BLOCK, rows), 0)
    query_at = lax.broadcasted_iota(jnp.int32, (BLOCK, rows), 1) // heads
    causal = key_at <= query_at

    def pair(qb, w):
        back = 7 + qb - w
        q = q_ref[pl.ds(qb * rows, rows), :]
        do = do_ref[pl.ds(qb * rows, rows), :]
        scores = dot(kw[pl.ds((w + 1) * BLOCK, BLOCK), :], q, NT)
        if back == 0:
            scores = jnp.where(causal, scores, MASKED)
        top = jnp.max(scores, axis=0, keepdims=True) * to_log2
        e = jnp.exp2(scores * to_log2 - top)
        dp = dot(vw[pl.ds((w + 1) * BLOCK, BLOCK), :], do, NT)
        at = w - qb
        e_ref[qb, pl.ds(at * BLOCK, BLOCK), :] = e
        dp_ref[qb, pl.ds(at * BLOCK, BLOCK), :] = dp
        bias = jnp.where(back <= before[qb], jnp.float32(0), jnp.float32(MASKED))
        stat[qb, 0, pl.ds(at, 1), :] = top + bias
        stat[qb, 1, pl.ds(at, 1), :] = jnp.sum(e, axis=0, keepdims=True)
        stat[qb, 2, pl.ds(at, 1), :] = jnp.sum(e * dp, axis=0, keepdims=True)

    pair(0, 7)
    pair(1, 7)
    pair(1, 8)
    for i in range(2):
        far_half(i, 1).wait_recv()

    @pl.when(core == 1)
    def _():
        for i in range(2):
            far_half(i, 0).wait_recv()
            across_far(i).start()

    for i in range(2):
        near(i).wait_recv()
        across_near(i).start()
    pair(0, 0)
    for w in (3, 4):
        pair(0, w)
        pair(1, w)
    for i in range(2):
        across_far(i).wait_recv()
        across_near(i).wait_recv()
    for w in (1, 2, 5, 6):
        pair(0, w)
        pair(1, w)

    factors, dots = [], []
    for qb in range(2):
        tops = stat[qb, 0]
        part = jnp.exp2(tops - jnp.max(tops, axis=0, keepdims=True))
        inv = 1.0 / jnp.sum(stat[qb, 1] * part, axis=0, keepdims=True)
        factors.append(part * inv)
        dots.append(jnp.sum(stat[qb, 2] * part, axis=0, keepdims=True) * inv)

    back_sends = []
    back_recv = {}

    def key_block(w):
        grads = [None, None]
        for qb in range(2):
            at = w - qb
            if not 0 <= at < REACH:
                continue
            probs = e_ref[qb, pl.ds(at * BLOCK, BLOCK), :] * factors[qb][at : at + 1]
            dscore = (probs * (dp_ref[qb, pl.ds(at * BLOCK, BLOCK), :] - dots[qb])).astype(jnp.bfloat16)
            ds_ref[qb, pl.ds(at * BLOCK, BLOCK), :] = dscore
            terms = (
                dot(dscore, q_ref[pl.ds(qb * rows, rows), :], NN),
                dot(probs.astype(jnp.bfloat16), do_ref[pl.ds(qb * rows, rows), :], NN),
            )
            grads = [t if g is None else g + t for g, t in zip(grads, terms)]
        grads[0] = grads[0] * scale
        d, half = (8 - w) // 2, (w + 1) % 2
        for i in range(2):
            sb[w, i] = grads[i].astype(jnp.bfloat16)
            if d == 0:
                own[i, pl.ds(half * BLOCK, BLOCK), :] = grads[i]
        for plane, row in enumerate((h, partner)):
            if d == 0 and plane == 0:
                continue
            which = role if plane == 0 else 1 - role
            copy = pltpu.make_async_remote_copy(
                src_ref=sb.at[w, which],
                dst_ref=rb.at[plane, d, pl.ds(half * BLOCK, BLOCK)],
                send_sem=b_send.at[plane, d, half],
                recv_sem=b_recv.at[plane, d, half],
                device_id=(ctx(-d), row),
                device_id_type=MESH,
            )
            copy.start()
            back_sends.append(copy)
            back_recv[plane, d, half] = copy

    for w in (1, 3, 5, 7, 0, 2, 4, 6, 8):
        key_block(w)

    for qb in range(2):
        grad = dot(kw[pl.ds((qb + 1) * BLOCK, REACH * BLOCK), :], ds_ref[qb], TN)
        dq_ref[pl.ds(qb * rows, rows), :] = (jnp.transpose(grad) * scale).astype(jnp.bfloat16)
    dq_copy = pltpu.make_async_copy(dq_ref, dq_out, out_sem.at[n_head])
    dq_copy.start()

    piece = shard // CHUNKS
    far = n_head // 2

    def row(distance, way):
        return lax.rem(h + n_head + distance * (1 - 2 * way), n_head)

    def hop(way, step, chunk):
        relay = (step - 1) // 2 * 2
        part = og.at[row(-relay, way), pl.ds(chunk * piece, piece)]
        return pltpu.make_async_remote_copy(
            src_ref=part,
            dst_ref=part,
            send_sem=c_send.at[way, step - 1, chunk],
            recv_sem=c_recv.at[way, step - 1, chunk],
            device_id=(s, row(step - relay, way)),
            device_id_type=MESH,
        )

    def steps(way, chunk):
        return far if chunk % 2 == way else n_head - 1 - far

    def pass_on(relay, way, chunk):
        for step in (relay + 2, relay + 1):
            if step <= steps(way, chunk):
                hop(way, step, chunk).start()

    for half in range(2):
        total = own[role, pl.ds(half * BLOCK, BLOCK), :]
        for (plane, d, at), copy in back_recv.items():
            if at == half:
                copy.wait_recv()
                total = total + rb[plane, d, pl.ds(half * BLOCK, BLOCK), :].astype(jnp.float32)
        og[h, pl.ds(half * BLOCK, BLOCK), :] = total.astype(jnp.bfloat16)
        for chunk in range(half * CHUNKS // 2, (half + 1) * CHUNKS // 2):
            for way in range(2):
                pass_on(0, way, chunk)

    outs = []

    def put(of, index):
        copy = pltpu.make_async_copy(og.at[of], kv_out.at[lax.rem(of, 2), of // 2], out_sem.at[index])
        copy.start()
        outs.append(copy)

    def arrive(step, way, chunk):
        if step <= steps(way, chunk):
            hop(way, step, chunk).wait_recv()

    put(h, 0)
    for step in (2, 4):
        for chunk in range(CHUNKS):
            for way in range(2):
                arrive(step, way, chunk)
                pass_on(step, way, chunk)
    for step in (2, 4, 1, 3, 5):
        for way in range(2):
            if step % 2:
                for chunk in range(CHUNKS):
                    arrive(step, way, chunk)
            put(row(-step, way), 2 * step - 1 + way)
    for chunk in range(CHUNKS):
        for way in range(2):
            arrive(far, way, chunk)
    put(row(far, 0), 2 * far - 1)

    for copy in back_sends:
        copy.wait_send()
    for i in range(2):
        far_half(i, 1).wait_send()
        near(i).wait_send()
        across_near(i).wait_send()
        across_own(i).wait_send()

    @pl.when(core == 1)
    def _():
        for i in range(2):
            far_half(i, 0).wait_send()

    for way in range(2):
        for chunk in range(CHUNKS):
            for step in range(1, steps(way, chunk) + 1):
                hop(way, step, chunk).wait_send()
    dq_copy.wait()
    for copy in outs:
        copy.wait()


def on_device(query_heads, key_head, value_head, out_grad, doc_blocks, n_ctx, n_head):
    tokens, heads, width = query_heads.shape
    kv_count = key_head.shape[1]
    rows = BLOCK * heads
    flat = lambda x: x.reshape(tokens * heads, width)
    dma = pltpu.SemaphoreType.DMA
    bf16, f32 = jnp.bfloat16, jnp.float32
    window = (REACH + 2) * BLOCK
    dq, kv = pl.pallas_call(
        functools.partial(kernel, n_ctx, n_head, heads, doc_blocks.shape[0]),
        out_shape=(
            jax.ShapeDtypeStruct((tokens * heads, width), bf16),
            jax.ShapeDtypeStruct((2, kv_count, tokens, width), bf16),
        ),
        in_specs=[pl.BlockSpec(memory_space=pl.ANY)] * 5,
        out_specs=(pl.BlockSpec(memory_space=pl.ANY),) * 2,
        scratch_shapes=[
            pltpu.SMEM(doc_blocks.shape, jnp.int32),
            pltpu.VMEM((tokens * heads, width), bf16),
            pltpu.VMEM((tokens * heads, width), bf16),
            pltpu.VMEM((window, width), bf16),
            pltpu.VMEM((window, width), bf16),
            pltpu.VMEM((2, REACH * BLOCK, rows), f32),
            pltpu.VMEM((2, REACH * BLOCK, rows), f32),
            pltpu.VMEM((2, 3, REACH, rows), f32),
            pltpu.VMEM((2, REACH * BLOCK, rows), bf16),
            pltpu.VMEM((2, 2 * BLOCK, width), f32),
            pltpu.VMEM((REACH + 1, 2, BLOCK, width), bf16),
            pltpu.VMEM((2, 5, 2 * BLOCK, width), bf16),
            pltpu.VMEM((n_head, tokens, width), bf16),
            pltpu.VMEM((tokens * heads, width), bf16),
            dma((5,)),
            dma((5, 2)),
            dma((5, 2)),
            dma((2, 5, 2)),
            dma((2, 5, 2)),
            dma((2, n_head // 2, CHUNKS)),
            dma((2, n_head // 2, CHUNKS)),
            dma((n_head + 1,)),
        ],
        compiler_params=pltpu.CompilerParams(
            collective_id=0, has_side_effects=True, vmem_limit_bytes=48 * 1024 * 1024
        ),
        name="attention_backward",
    )(
        *(
            pltpu.with_memory_space_constraint(x, pltpu.HBM)
            for x in (
                doc_blocks,
                flat(query_heads),
                flat(out_grad),
                jnp.transpose(key_head, (1, 0, 2)),
                jnp.transpose(value_head, (1, 0, 2)),
            )
        )
    )
    kv = jnp.transpose(kv, (0, 2, 1, 3))
    return dq.reshape(tokens, heads, width), kv[0], kv[1]


def solution(mesh):
    return jax.shard_map(
        functools.partial(on_device, n_ctx=mesh.shape["ctx"], n_head=mesh.shape["head"]),
        mesh=mesh,
        in_specs=(
            P("ctx", "head", None),
            P("ctx", None, None),
            P("ctx", None, None),
            P("ctx", "head", None),
            P(),
        ),
        out_specs=(P("ctx", "head", None), P("ctx", None, None), P("ctx", None, None)),
        check_vma=False,
    )
```

```python
import functools

import jax
import jax.numpy as jnp
from jax import lax
from jax.experimental import pallas as pl
from jax.experimental.pallas import tpu as pltpu
from jax.sharding import PartitionSpec as P

GROUP = 8
BLOCK = 128
REACH = 8
MASKED = -1e30
LOG2E = 1.4426950408889634
MESH = pl.DeviceIdType.MESH
CHUNKS = 4

NT = (((1,), (1,)), ((), ()))
NN = (((1,), (0,)), ((), ()))
TN = (((0,), (0,)), ((), ()))


def dot(a, b, dims):
    return lax.dot_general(a, b, dims, preferred_element_type=jnp.float32)


def kernel(
    n_ctx, n_head, heads, docs,
    docs_hbm, q_hbm, do_hbm, k_hbm, v_hbm,
    dq_out, kv_out,
    docs_ref, q_ref, do_ref, kw, vw, e_ref, dp_ref, stat, ds_ref, own, hold, xs, xr, sums, rb, og, dq_ref,
    load_sem, a_send, a_recv, x_send, x_recv, b_send, b_recv, c_send, c_recv, out_sem,
):
    width = q_ref.shape[1]
    shard = 2 * BLOCK
    rows = BLOCK * heads
    scale = width ** -0.5
    to_log2 = scale * LOG2E
    s = lax.axis_index("ctx")
    h = lax.axis_index("head")
    role = lax.rem(h, 2)
    partner = h + 1 - 2 * role
    group = h * heads // GROUP

    core = lax.rem(s, 2)
    sibling = s + 1 - 2 * core

    def ctx(delta):
        return lax.rem(s + delta + n_ctx, n_ctx)

    def slot(d, first=0, size=shard):
        return pl.ds((8 - 2 * d) * BLOCK + first, size)

    loads = [
        pltpu.make_async_copy(k_hbm.at[group], kw.at[slot(0)], load_sem.at[0]),
        pltpu.make_async_copy(v_hbm.at[group], vw.at[slot(0)], load_sem.at[1]),
        pltpu.make_async_copy(q_hbm, q_ref, load_sem.at[2]),
        pltpu.make_async_copy(do_hbm, do_ref, load_sem.at[3]),
        pltpu.make_async_copy(docs_hbm, docs_ref, load_sem.at[4]),
    ]
    for copy in loads:
        copy.start()

    barrier = pltpu.get_barrier_semaphore()
    near_rows = [(s, lax.rem(h + n_head + d, n_head)) for d in (-2, -1, 1, 2)]
    peers = [(ctx(-4), h), (ctx(-2), h), (sibling, h)] + near_rows
    for peer in peers:
        pl.semaphore_signal(barrier, inc=1, device_id=peer, device_id_type=MESH)
    pl.semaphore_wait(barrier, len(peers))

    pairs = ((k_hbm, kw), (v_hbm, vw))

    def push(i, src, dst, sem, target):
        return pltpu.make_async_remote_copy(
            src_ref=src,
            dst_ref=dst,
            send_sem=a_send.at[sem, i],
            recv_sem=a_recv.at[sem, i],
            device_id=(target, h),
            device_id_type=MESH,
        )

    def far_half(i, half):
        src, dst = pairs[i]
        at = half * BLOCK
        return push(i, src.at[group, pl.ds(at, BLOCK)], dst.at[slot(4, at, BLOCK)], half, ctx(4))

    def near(i):
        src, dst = pairs[i]
        return push(i, src.at[group], dst.at[slot(2)], 2, ctx(2))

    def across_near(i):
        dst = pairs[i][1]
        to = pl.ds((2 + 4 * core) * BLOCK, shard)
        return push(i, dst.at[slot(2)], dst.at[to], 3, sibling)

    def across_own(i):
        src, dst = pairs[i]
        return push(i, src.at[group], dst.at[slot(1)], 4, sibling)

    def across_far(i):
        dst = pairs[i][1]
        return push(i, dst.at[slot(4)], dst.at[slot(3)], 4, sibling)

    for i in range(2):
        far_half(i, 1).start()

    @pl.when(core == 1)
    def _():
        for i in range(2):
            far_half(i, 0).start()

    for i in range(2):
        near(i).start()

    @pl.when(core == 0)
    def _():
        for i in range(2):
            across_own(i).start()

    for copy in loads:
        copy.wait()

    before = []
    for qb in range(2):
        at = 2 * s + qb
        total = jnp.int32(0)
        start = jnp.int32(0)
        for i in range(docs):
            start = jnp.where(total <= at, total, start)
            total = total + docs_ref[i]
        before.append(at - start)

    key_at = lax.broadcasted_iota(jnp.int32, (BLOCK, rows), 0)
    query_at = lax.broadcasted_iota(jnp.int32, (BLOCK, rows), 1) // heads
    causal = key_at <= query_at

    def pair(qb, w):
        back = 7 + qb - w
        q = q_ref[pl.ds(qb * rows, rows), :]
        do = do_ref[pl.ds(qb * rows, rows), :]
        keys = pl.ds(pl.multiple_of((w + 1) * BLOCK, BLOCK), BLOCK)
        scores = dot(kw[keys, :], q, NT)
        if isinstance(w, int) and back == 0:
            scores = jnp.where(causal, scores, MASKED)
        top = jnp.max(scores, axis=0, keepdims=True) * to_log2
        e = jnp.exp2(scores * to_log2 - top)
        dp = dot(vw[keys, :], do, NT)
        at = w - qb
        tile = pl.ds(pl.multiple_of(at * BLOCK, BLOCK), BLOCK)
        e_ref[qb, tile, :] = e
        dp_ref[qb, tile, :] = dp
        bias = jnp.where(back <= before[qb], jnp.float32(0), jnp.float32(MASKED))
        stat[qb, 0, pl.ds(at, 1), :] = top + bias
        stat[qb, 1, pl.ds(at, 1), :] = jnp.sum(e, axis=0, keepdims=True)
        stat[qb, 2, pl.ds(at, 1), :] = jnp.sum(e * dp, axis=0, keepdims=True)

    pair(0, 7)
    pair(1, 7)
    pair(1, 8)
    for i in range(2):
        far_half(i, 1).wait_recv()

    @pl.when(core == 1)
    def _():
        for i in range(2):
            far_half(i, 0).wait_recv()
            across_far(i).start()

    for i in range(2):
        near(i).wait_recv()
        across_near(i).start()
    pair(0, 0)
    for w in (3, 4):
        pair(0, w)
        pair(1, w)
    for brought, first in ((across_far, 1 + 4 * core), (across_near, 5 - 4 * core)):
        for i in range(2):
            brought(i).wait_recv()
        for w in (first, first + 1):
            pair(0, w)
            pair(1, w)

    factors, dots = [], []
    for qb in range(2):
        tops = stat[qb, 0]
        part = jnp.exp2(tops - jnp.max(tops, axis=0, keepdims=True))
        inv = 1.0 / jnp.sum(stat[qb, 1] * part, axis=0, keepdims=True)
        factors.append(part * inv)
        dots.append(jnp.sum(stat[qb, 2] * part, axis=0, keepdims=True) * inv)

    def key_block(w):
        grads = [None, None]
        for qb in range(2):
            at = w - qb
            if not 0 <= at < REACH:
                continue
            probs = e_ref[qb, pl.ds(at * BLOCK, BLOCK), :] * factors[qb][at : at + 1]
            dscore = (probs * (dp_ref[qb, pl.ds(at * BLOCK, BLOCK), :] - dots[qb])).astype(jnp.bfloat16)
            ds_ref[qb, pl.ds(at * BLOCK, BLOCK), :] = dscore
            terms = (
                dot(dscore, q_ref[pl.ds(qb * rows, rows), :], NN),
                dot(probs.astype(jnp.bfloat16), do_ref[pl.ds(qb * rows, rows), :], NN),
            )
            grads = [t if g is None else g + t for g, t in zip(grads, terms)]
        return grads[0] * scale, grads[1]

    def across(i):
        return pltpu.make_async_remote_copy(
            src_ref=xs.at[i],
            dst_ref=xr.at[i],
            send_sem=x_send.at[i],
            recv_sem=x_recv.at[i],
            device_id=(sibling, h),
            device_id_type=MESH,
        )

    def back(chips, half, plane):
        which = role if plane == 0 else 1 - role
        src = xr.at[0, which] if (chips, half) == (2, 0) else sums.at[chips, half, which]
        return pltpu.make_async_remote_copy(
            src_ref=src,
            dst_ref=rb.at[plane, chips, pl.ds(half * BLOCK, BLOCK)],
            send_sem=b_send.at[plane, chips, half],
            recv_sem=b_recv.at[plane, chips, half],
            device_id=(ctx(-2 * chips), h if plane == 0 else partner),
            device_id_type=MESH,
        )

    for i, w in enumerate((1, 2, 5, 6)):
        for kind, grad in enumerate(key_block(w)):
            xs[i, kind] = grad.astype(jnp.bfloat16)
        across(i).start()
    for i, w in enumerate((0, 3, 4)):
        for kind, grad in enumerate(key_block(w)):
            hold[i, kind] = grad

    def crossed(i, kind):
        return xr[i, kind].astype(jnp.float32)

    across(0).wait_recv()

    @pl.when(core == 1)
    def _():
        for plane in range(2):
            back(2, 0, plane).start()

    across(1).wait_recv()
    for kind in range(2):
        sums[2, 1, kind] = (hold[0, kind] + jnp.where(core == 1, crossed(1, kind), 0.0)).astype(jnp.bfloat16)
    for plane in range(2):
        back(2, 1, plane).start()
    across(2).wait_recv()
    across(3).wait_recv()
    for half in range(2):
        for kind in range(2):
            sums[1, half, kind] = (hold[1 + half, kind] + crossed(half + 2 * core, kind)).astype(jnp.bfloat16)
        for plane in range(2):
            back(1, half, plane).start()
    for half in range(2):
        for kind, grad in enumerate(key_block(7 + half)):
            grad = grad + jnp.where(core == 0, crossed(2 + half, kind), 0.0)
            own[kind, pl.ds(half * BLOCK, BLOCK), :] = grad
            sums[0, half, kind] = grad.astype(jnp.bfloat16)
        back(0, half, 1).start()

    for qb in range(2):
        grad = dot(kw[pl.ds((qb + 1) * BLOCK, REACH * BLOCK), :], ds_ref[qb], TN)
        dq_ref[pl.ds(qb * rows, rows), :] = (jnp.transpose(grad) * scale).astype(jnp.bfloat16)
    dq_copy = pltpu.make_async_copy(dq_ref, dq_out, out_sem.at[n_head])
    dq_copy.start()

    piece = shard // CHUNKS
    far = n_head // 2

    def row(distance, way):
        return lax.rem(h + n_head + distance * (1 - 2 * way), n_head)

    def hop(way, step, chunk):
        relay = (step - 1) // 2 * 2
        part = og.at[row(-relay, way), pl.ds(chunk * piece, piece)]
        return pltpu.make_async_remote_copy(
            src_ref=part,
            dst_ref=part,
            send_sem=c_send.at[way, step - 1, chunk],
            recv_sem=c_recv.at[way, step - 1, chunk],
            device_id=(s, row(step - relay, way)),
            device_id_type=MESH,
        )

    def steps(way, chunk):
        return far if chunk % 2 == way else n_head - 1 - far

    def pass_on(relay, way, chunk):
        for step in (relay + 2, relay + 1):
            if step <= steps(way, chunk):
                hop(way, step, chunk).start()

    @pl.when(core == 1)
    def _():
        for plane in range(2):
            back(2, 0, plane).wait_recv()
            own[role, pl.ds(0, BLOCK), :] += rb[plane, 2, pl.ds(0, BLOCK), :].astype(jnp.float32)

    for half in range(2):
        total = own[role, pl.ds(half * BLOCK, BLOCK), :]
        for chips, plane in ((0, 1), (1, 0), (1, 1)) + ((2, 0), (2, 1)) * half:
            back(chips, half, plane).wait_recv()
            total = total + rb[plane, chips, pl.ds(half * BLOCK, BLOCK), :].astype(jnp.float32)
        og[h, pl.ds(half * BLOCK, BLOCK), :] = total.astype(jnp.bfloat16)
        for chunk in range(half * CHUNKS // 2, (half + 1) * CHUNKS // 2):
            for way in range(2):
                pass_on(0, way, chunk)

    outs = []

    def put(of, index):
        copy = pltpu.make_async_copy(og.at[of], kv_out.at[lax.rem(of, 2), of // 2], out_sem.at[index])
        copy.start()
        outs.append(copy)

    def arrive(step, way, chunk):
        if step <= steps(way, chunk):
            hop(way, step, chunk).wait_recv()

    put(h, 0)
    for step in (2, 4):
        for chunk in range(CHUNKS):
            for way in range(2):
                arrive(step, way, chunk)
                pass_on(step, way, chunk)
    for step in (2, 4, 1, 3, 5):
        for way in range(2):
            if step % 2:
                for chunk in range(CHUNKS):
                    arrive(step, way, chunk)
            put(row(-step, way), 2 * step - 1 + way)
    for chunk in range(CHUNKS):
        for way in range(2):
            arrive(far, way, chunk)
    put(row(far, 0), 2 * far - 1)

    for i in range(4):
        across(i).wait_send()
    for half in range(2):
        for chips, plane in ((0, 1), (1, 0), (1, 1)) + ((2, 0), (2, 1)) * half:
            back(chips, half, plane).wait_send()
    for i in range(2):
        far_half(i, 1).wait_send()
        near(i).wait_send()
        across_near(i).wait_send()
        across_own(i).wait_send()

    @pl.when(core == 1)
    def _():
        for i in range(2):
            far_half(i, 0).wait_send()
            back(2, 0, i).wait_send()

    for way in range(2):
        for chunk in range(CHUNKS):
            for step in range(1, steps(way, chunk) + 1):
                hop(way, step, chunk).wait_send()
    dq_copy.wait()
    for copy in outs:
        copy.wait()


def copy_out(dq, kv, dq_out, dk_out, dv_out, sems):
    copies = [
        pltpu.make_async_copy(kv.at[0], dk_out, sems.at[0]),
        pltpu.make_async_copy(kv.at[1], dv_out, sems.at[1]),
        pltpu.make_async_copy(dq, dq_out, sems.at[2]),
    ]
    for copy in copies:
        copy.start()
    for copy in copies:
        copy.wait()


def on_device(query_heads, key_head, value_head, out_grad, doc_blocks, n_ctx, n_head):
    tokens, heads, width = query_heads.shape
    kv_count = key_head.shape[1]
    rows = BLOCK * heads
    flat = lambda x: x.reshape(tokens * heads, width)
    dma = pltpu.SemaphoreType.DMA
    bf16, f32 = jnp.bfloat16, jnp.float32
    window = (REACH + 2) * BLOCK
    dq, kv = pl.pallas_call(
        functools.partial(kernel, n_ctx, n_head, heads, doc_blocks.shape[0]),
        out_shape=(
            jax.ShapeDtypeStruct((tokens * heads, width), bf16),
            jax.ShapeDtypeStruct((2, kv_count, tokens, width), bf16),
        ),
        in_specs=[pl.BlockSpec(memory_space=pl.ANY)] * 5,
        out_specs=(pl.BlockSpec(memory_space=pl.ANY),) * 2,
        scratch_shapes=[
            pltpu.SMEM(doc_blocks.shape, jnp.int32),
            pltpu.VMEM((tokens * heads, width), bf16),
            pltpu.VMEM((tokens * heads, width), bf16),
            pltpu.VMEM((window, width), bf16),
            pltpu.VMEM((window, width), bf16),
            pltpu.VMEM((2, REACH * BLOCK, rows), f32),
            pltpu.VMEM((2, REACH * BLOCK, rows), f32),
            pltpu.VMEM((2, 3, REACH, rows), f32),
            pltpu.VMEM((2, REACH * BLOCK, rows), bf16),
            pltpu.VMEM((2, 2 * BLOCK, width), f32),
            pltpu.VMEM((3, 2, BLOCK, width), f32),
            pltpu.VMEM((4, 2, BLOCK, width), bf16),
            pltpu.VMEM((4, 2, BLOCK, width), bf16),
            pltpu.VMEM((3, 2, 2, BLOCK, width), bf16),
            pltpu.VMEM((2, 3, 2 * BLOCK, width), bf16),
            pltpu.VMEM((n_head, tokens, width), bf16),
            pltpu.VMEM((tokens * heads, width), bf16),
            dma((5,)),
            dma((5, 2)),
            dma((5, 2)),
            dma((4,)),
            dma((4,)),
            dma((2, 3, 2)),
            dma((2, 3, 2)),
            dma((2, n_head // 2, CHUNKS)),
            dma((2, n_head // 2, CHUNKS)),
            dma((n_head + 1,)),
        ],
        compiler_params=pltpu.CompilerParams(
            collective_id=0, has_side_effects=True, vmem_limit_bytes=48 * 1024 * 1024
        ),
        name="attention_backward",
    )(
        *(
            pltpu.with_memory_space_constraint(x, pltpu.HBM)
            for x in (
                doc_blocks,
                flat(query_heads),
                flat(out_grad),
                jnp.transpose(key_head, (1, 0, 2)),
                jnp.transpose(value_head, (1, 0, 2)),
            )
        )
    )
    any_space = pl.BlockSpec(memory_space=pl.ANY)
    dq, dk, dv = pl.pallas_call(
        copy_out,
        out_shape=(
            jax.ShapeDtypeStruct(dq.shape, bf16),
            jax.ShapeDtypeStruct(kv.shape[1:], bf16),
            jax.ShapeDtypeStruct(kv.shape[1:], bf16),
        ),
        in_specs=[any_space] * 2,
        out_specs=(any_space,) * 3,
        scratch_shapes=[dma((3,))],
        compiler_params=pltpu.CompilerParams(vmem_limit_bytes=8 * 1024 * 1024),
        name="copy_out",
    )(dq, kv)
    return (
        dq.reshape(tokens, heads, width),
        jnp.transpose(dk, (1, 0, 2)),
        jnp.transpose(dv, (1, 0, 2)),
    )


def solution(mesh):
    return jax.shard_map(
        functools.partial(on_device, n_ctx=mesh.shape["ctx"], n_head=mesh.shape["head"]),
        mesh=mesh,
        in_specs=(
            P("ctx", "head", None),
            P("ctx", None, None),
            P("ctx", None, None),
            P("ctx", "head", None),
            P(),
        ),
        out_specs=(P("ctx", "head", None), P("ctx", None, None), P("ctx", None, None)),
        check_vma=False,
    )
```

```python
import functools

import jax
import jax.numpy as jnp
from jax import lax
from jax.experimental import pallas as pl
from jax.experimental.pallas import tpu as pltpu
from jax.sharding import PartitionSpec as P

GROUP = 8
BLOCK = 128
REACH = 8
MASKED = -1e30
LOG2E = 1.4426950408889634
MESH = pl.DeviceIdType.MESH
CHUNKS = 2
RELAYS = (2, 4)

NT = (((1,), (1,)), ((), ()))
NN = (((1,), (0,)), ((), ()))
TN = (((0,), (0,)), ((), ()))


def dot(a, b, dims):
    return lax.dot_general(a, b, dims, preferred_element_type=jnp.float32)


def kernel(
    n_ctx, n_head, heads, docs,
    docs_hbm, q_hbm, do_hbm, k_hbm, v_hbm,
    dq_out, kv_out,
    docs_ref, q_ref, do_ref, kw, vw, e_ref, dp_ref, stat, ds_ref, own, hold, xs, xr, sums, rb, total_ref, dq_ref,
    load_sem, a_send, a_recv, x_send, x_recv, b_send, b_recv, c_send, c_recv, out_sem,
):
    width = q_ref.shape[1]
    shard = 2 * BLOCK
    rows = BLOCK * heads
    scale = width ** -0.5
    to_log2 = scale * LOG2E
    s = lax.axis_index("ctx")
    h = lax.axis_index("head")
    role = lax.rem(h, 2)
    partner = h + 1 - 2 * role
    group = h * heads // GROUP

    core = lax.rem(s, 2)
    sibling = s + 1 - 2 * core

    def ctx(delta):
        return lax.rem(s + delta + n_ctx, n_ctx)

    def slot(d, first=0, size=shard):
        return pl.ds((8 - 2 * d) * BLOCK + first, size)

    loads = [
        pltpu.make_async_copy(k_hbm.at[group], kw.at[slot(0)], load_sem.at[0]),
        pltpu.make_async_copy(v_hbm.at[group], vw.at[slot(0)], load_sem.at[1]),
        pltpu.make_async_copy(q_hbm, q_ref, load_sem.at[2]),
        pltpu.make_async_copy(do_hbm, do_ref, load_sem.at[3]),
        pltpu.make_async_copy(docs_hbm, docs_ref, load_sem.at[4]),
    ]
    for copy in loads:
        copy.start()

    barrier = pltpu.get_barrier_semaphore()
    near_rows = [(s, lax.rem(h + n_head + d, n_head)) for d in (-2, -1, 1, 2)]
    peers = [(ctx(-4), h), (ctx(-2), h), (sibling, h)] + near_rows
    for peer in peers:
        pl.semaphore_signal(barrier, inc=1, device_id=peer, device_id_type=MESH)
    pl.semaphore_wait(barrier, len(peers))

    pairs = ((k_hbm, kw), (v_hbm, vw))

    def push(i, src, dst, sem, target):
        return pltpu.make_async_remote_copy(
            src_ref=src,
            dst_ref=dst,
            send_sem=a_send.at[sem, i],
            recv_sem=a_recv.at[sem, i],
            device_id=(target, h),
            device_id_type=MESH,
        )

    def far_half(i, half):
        src, dst = pairs[i]
        at = half * BLOCK
        return push(i, src.at[group, pl.ds(at, BLOCK)], dst.at[slot(4, at, BLOCK)], half, ctx(4))

    def near(i):
        src, dst = pairs[i]
        return push(i, src.at[group], dst.at[slot(2)], 2, ctx(2))

    def across_near(i):
        dst = pairs[i][1]
        to = pl.ds((2 + 4 * core) * BLOCK, shard)
        return push(i, dst.at[slot(2)], dst.at[to], 3, sibling)

    def across_own(i):
        src, dst = pairs[i]
        return push(i, src.at[group], dst.at[slot(1)], 4, sibling)

    def across_far(i):
        dst = pairs[i][1]
        return push(i, dst.at[slot(4)], dst.at[slot(3)], 4, sibling)

    for i in range(2):
        far_half(i, 1).start()

    @pl.when(core == 1)
    def _():
        for i in range(2):
            far_half(i, 0).start()

    for i in range(2):
        near(i).start()

    @pl.when(core == 0)
    def _():
        for i in range(2):
            across_own(i).start()

    for copy in loads:
        copy.wait()

    before = []
    for qb in range(2):
        at = 2 * s + qb
        total = jnp.int32(0)
        start = jnp.int32(0)
        for i in range(docs):
            start = jnp.where(total <= at, total, start)
            total = total + docs_ref[i]
        before.append(at - start)

    key_at = lax.broadcasted_iota(jnp.int32, (BLOCK, rows), 0)
    query_at = lax.broadcasted_iota(jnp.int32, (BLOCK, rows), 1) // heads
    causal = key_at <= query_at

    def pair(qb, w):
        back = 7 + qb - w
        q = q_ref[pl.ds(qb * rows, rows), :]
        do = do_ref[pl.ds(qb * rows, rows), :]
        keys = pl.ds(pl.multiple_of((w + 1) * BLOCK, BLOCK), BLOCK)
        scores = dot(kw[keys, :], q, NT)
        if isinstance(w, int) and back == 0:
            scores = jnp.where(causal, scores, MASKED)
        top = jnp.max(scores, axis=0, keepdims=True) * to_log2
        e = jnp.exp2(scores * to_log2 - top)
        dp = dot(vw[keys, :], do, NT)
        at = w - qb
        tile = pl.ds(pl.multiple_of(at * BLOCK, BLOCK), BLOCK)
        e_ref[qb, tile, :] = e
        dp_ref[qb, tile, :] = dp
        bias = jnp.where(back <= before[qb], jnp.float32(0), jnp.float32(MASKED))
        stat[qb, 0, pl.ds(at, 1), :] = top + bias
        stat[qb, 1, pl.ds(at, 1), :] = jnp.sum(e, axis=0, keepdims=True)
        stat[qb, 2, pl.ds(at, 1), :] = jnp.sum(e * dp, axis=0, keepdims=True)

    pair(0, 7)
    pair(1, 7)
    pair(1, 8)
    for i in range(2):
        far_half(i, 1).wait_recv()

    @pl.when(core == 1)
    def _():
        for i in range(2):
            far_half(i, 0).wait_recv()
            across_far(i).start()

    for i in range(2):
        near(i).wait_recv()
        across_near(i).start()
    pair(0, 0)
    for w in (3, 4):
        pair(0, w)
        pair(1, w)
    for brought, first in ((across_far, 1 + 4 * core), (across_near, 5 - 4 * core)):
        for i in range(2):
            brought(i).wait_recv()
        for w in (first, first + 1):
            pair(0, w)
            pair(1, w)

    factors, dots = [], []
    for qb in range(2):
        tops = stat[qb, 0]
        part = jnp.exp2(tops - jnp.max(tops, axis=0, keepdims=True))
        inv = 1.0 / jnp.sum(stat[qb, 1] * part, axis=0, keepdims=True)
        factors.append(part * inv)
        dots.append(jnp.sum(stat[qb, 2] * part, axis=0, keepdims=True) * inv)

    def key_block(w):
        grads = [None, None]
        for qb in range(2):
            at = w - qb
            if not 0 <= at < REACH:
                continue
            probs = e_ref[qb, pl.ds(at * BLOCK, BLOCK), :] * factors[qb][at : at + 1]
            dscore = (probs * (dp_ref[qb, pl.ds(at * BLOCK, BLOCK), :] - dots[qb])).astype(jnp.bfloat16)
            ds_ref[qb, pl.ds(at * BLOCK, BLOCK), :] = dscore
            terms = (
                dot(dscore, q_ref[pl.ds(qb * rows, rows), :], NN),
                dot(probs.astype(jnp.bfloat16), do_ref[pl.ds(qb * rows, rows), :], NN),
            )
            grads = [t if g is None else g + t for g, t in zip(grads, terms)]
        return grads[0] * scale, grads[1]

    def across(i):
        return pltpu.make_async_remote_copy(
            src_ref=xs.at[i],
            dst_ref=xr.at[i],
            send_sem=x_send.at[i],
            recv_sem=x_recv.at[i],
            device_id=(sibling, h),
            device_id_type=MESH,
        )

    def back(chips, half, plane):
        which = role if plane == 0 else 1 - role
        src = xr.at[0, which] if (chips, half) == (2, 0) else sums.at[chips, half, which]
        return pltpu.make_async_remote_copy(
            src_ref=src,
            dst_ref=rb.at[plane, chips, pl.ds(half * BLOCK, BLOCK)],
            send_sem=b_send.at[plane, chips, half],
            recv_sem=b_recv.at[plane, chips, half],
            device_id=(ctx(-2 * chips), h if plane == 0 else partner),
            device_id_type=MESH,
        )

    for i, w in enumerate((1, 2, 5, 6)):
        for kind, grad in enumerate(key_block(w)):
            xs[i, kind] = grad.astype(jnp.bfloat16)
        across(i).start()
    for i, w in enumerate((0, 3, 4)):
        for kind, grad in enumerate(key_block(w)):
            hold[i, kind] = grad

    def crossed(i, kind):
        return xr[i, kind].astype(jnp.float32)

    across(0).wait_recv()

    @pl.when(core == 1)
    def _():
        for plane in range(2):
            back(2, 0, plane).start()

    across(2).wait_recv()

    def near_sum(half):
        for kind in range(2):
            sums[1, half, kind] = (hold[1 + half, kind] + crossed(half + 2 * core, kind)).astype(jnp.bfloat16)
        for plane in range(2):
            back(1, half, plane).start()

    near_sum(0)
    across(1).wait_recv()
    for kind in range(2):
        sums[2, 1, kind] = (hold[0, kind] + jnp.where(core == 1, crossed(1, kind), 0.0)).astype(jnp.bfloat16)
    for plane in range(2):
        back(2, 1, plane).start()
    across(3).wait_recv()
    near_sum(1)
    for half in range(2):
        for kind, grad in enumerate(key_block(7 + half)):
            grad = grad + jnp.where(core == 0, crossed(2 + half, kind), 0.0)
            own[kind, pl.ds(half * BLOCK, BLOCK), :] = grad
            sums[0, half, kind] = grad.astype(jnp.bfloat16)
        back(0, half, 1).start()

    for qb in range(2):
        grad = dot(kw[pl.ds((qb + 1) * BLOCK, REACH * BLOCK), :], ds_ref[qb], TN)
        dq_ref[pl.ds(qb * rows, rows), :] = (jnp.transpose(grad) * scale).astype(jnp.bfloat16)
    dq_copy = pltpu.make_async_copy(dq_ref, dq_out, out_sem.at[0])
    dq_copy.start()

    piece = shard // CHUNKS
    far = n_head // 2

    def row(distance, way):
        return lax.rem(h + n_head + distance * (1 - 2 * way), n_head)

    def hop(way, step, chunk):
        relay = (step - 1) // 2 * 2
        rows_of = pl.ds(chunk * piece, piece)
        part = kv_out.at[row(-relay, way), rows_of]
        return pltpu.make_async_remote_copy(
            src_ref=part if relay else total_ref.at[rows_of],
            dst_ref=part,
            send_sem=c_send.at[way, step - 1, chunk],
            recv_sem=c_recv.at[way, step - 1, chunk],
            device_id=(s, row(step - relay, way)),
            device_id_type=MESH,
        )

    def steps(way, chunk):
        return far if chunk % 2 == way else n_head - 1 - far

    def pass_on(relay, way, chunk):
        for step in (relay + 2, relay + 1):
            if step <= steps(way, chunk):
                hop(way, step, chunk).start()

    @pl.when(core == 1)
    def _():
        for plane in range(2):
            back(2, 0, plane).wait_recv()
            own[role, pl.ds(0, BLOCK), :] += rb[plane, 2, pl.ds(0, BLOCK), :].astype(jnp.float32)

    for half in range(2):
        total = own[role, pl.ds(half * BLOCK, BLOCK), :]
        for chips, plane in ((0, 1), (1, 0), (1, 1)) + ((2, 0), (2, 1)) * half:
            back(chips, half, plane).wait_recv()
            total = total + rb[plane, chips, pl.ds(half * BLOCK, BLOCK), :].astype(jnp.float32)
        total_ref[pl.ds(half * BLOCK, BLOCK), :] = total.astype(jnp.bfloat16)
        for chunk in range(half * CHUNKS // 2, (half + 1) * CHUNKS // 2):
            for way in range(2):
                pass_on(0, way, chunk)

    total_copy = pltpu.make_async_copy(total_ref, kv_out.at[h], out_sem.at[1])
    total_copy.start()
    for step in RELAYS:
        for chunk in range(CHUNKS):
            for way in range(2):
                hop(way, step, chunk).wait_recv()
                pass_on(step, way, chunk)
    for way in range(2):
        for chunk in range(CHUNKS):
            for step in range(1, steps(way, chunk) + 1):
                if step not in RELAYS:
                    hop(way, step, chunk).wait_recv()

    for i in range(4):
        across(i).wait_send()
    for half in range(2):
        for chips, plane in ((0, 1), (1, 0), (1, 1)) + ((2, 0), (2, 1)) * half:
            back(chips, half, plane).wait_send()
    for i in range(2):
        far_half(i, 1).wait_send()
        near(i).wait_send()
        across_near(i).wait_send()
        across_own(i).wait_send()

    @pl.when(core == 1)
    def _():
        for i in range(2):
            far_half(i, 0).wait_send()
            back(2, 0, i).wait_send()

    for way in range(2):
        for chunk in range(CHUNKS):
            for step in range(1, steps(way, chunk) + 1):
                hop(way, step, chunk).wait_send()
    dq_copy.wait()
    total_copy.wait()


def copy_out(dq, kv, dq_out, dk_out, dv_out, sems):
    copies = [
        pltpu.make_async_copy(kv.at[:, 0], dk_out, sems.at[0]),
        pltpu.make_async_copy(kv.at[:, 1], dv_out, sems.at[1]),
        pltpu.make_async_copy(dq, dq_out, sems.at[2]),
    ]
    for copy in copies:
        copy.start()
    for copy in copies:
        copy.wait()


def on_device(query_heads, key_head, value_head, out_grad, doc_blocks, n_ctx, n_head):
    tokens, heads, width = query_heads.shape
    kv_count = key_head.shape[1]
    rows = BLOCK * heads
    flat = lambda x: x.reshape(tokens * heads, width)
    dma = pltpu.SemaphoreType.DMA
    bf16, f32 = jnp.bfloat16, jnp.float32
    window = (REACH + 2) * BLOCK
    dq, kv = pl.pallas_call(
        functools.partial(kernel, n_ctx, n_head, heads, doc_blocks.shape[0]),
        out_shape=(
            jax.ShapeDtypeStruct((tokens * heads, width), bf16),
            jax.ShapeDtypeStruct((n_head, tokens, width), bf16),
        ),
        in_specs=[pl.BlockSpec(memory_space=pl.ANY)] * 5,
        out_specs=(pl.BlockSpec(memory_space=pl.ANY),) * 2,
        scratch_shapes=[
            pltpu.SMEM(doc_blocks.shape, jnp.int32),
            pltpu.VMEM((tokens * heads, width), bf16),
            pltpu.VMEM((tokens * heads, width), bf16),
            pltpu.VMEM((window, width), bf16),
            pltpu.VMEM((window, width), bf16),
            pltpu.VMEM((2, REACH * BLOCK, rows), f32),
            pltpu.VMEM((2, REACH * BLOCK, rows), f32),
            pltpu.VMEM((2, 3, REACH, rows), f32),
            pltpu.VMEM((2, REACH * BLOCK, rows), bf16),
            pltpu.VMEM((2, 2 * BLOCK, width), f32),
            pltpu.VMEM((3, 2, BLOCK, width), f32),
            pltpu.VMEM((4, 2, BLOCK, width), bf16),
            pltpu.VMEM((4, 2, BLOCK, width), bf16),
            pltpu.VMEM((3, 2, 2, BLOCK, width), bf16),
            pltpu.VMEM((2, 3, 2 * BLOCK, width), bf16),
            pltpu.VMEM((tokens, width), bf16),
            pltpu.VMEM((tokens * heads, width), bf16),
            dma((5,)),
            dma((5, 2)),
            dma((5, 2)),
            dma((4,)),
            dma((4,)),
            dma((2, 3, 2)),
            dma((2, 3, 2)),
            dma((2, n_head // 2, CHUNKS)),
            dma((2, n_head // 2, CHUNKS)),
            dma((2,)),
        ],
        compiler_params=pltpu.CompilerParams(
            collective_id=0, has_side_effects=True, vmem_limit_bytes=48 * 1024 * 1024
        ),
        name="attention_backward",
    )(
        *(
            pltpu.with_memory_space_constraint(x, pltpu.HBM)
            for x in (
                doc_blocks,
                flat(query_heads),
                flat(out_grad),
                jnp.transpose(key_head, (1, 0, 2)),
                jnp.transpose(value_head, (1, 0, 2)),
            )
        )
    )
    any_space = pl.BlockSpec(memory_space=pl.ANY)
    dq, dk, dv = pl.pallas_call(
        copy_out,
        out_shape=(
            jax.ShapeDtypeStruct(dq.shape, bf16),
            jax.ShapeDtypeStruct((kv_count, tokens, width), bf16),
            jax.ShapeDtypeStruct((kv_count, tokens, width), bf16),
        ),
        in_specs=[any_space] * 2,
        out_specs=(any_space,) * 3,
        scratch_shapes=[dma((3,))],
        compiler_params=pltpu.CompilerParams(vmem_limit_bytes=8 * 1024 * 1024),
        name="copy_out",
    )(dq, kv.reshape(kv_count, 2, tokens, width))
    return (
        dq.reshape(tokens, heads, width),
        jnp.transpose(dk, (1, 0, 2)),
        jnp.transpose(dv, (1, 0, 2)),
    )


def solution(mesh):
    return jax.shard_map(
        functools.partial(on_device, n_ctx=mesh.shape["ctx"], n_head=mesh.shape["head"]),
        mesh=mesh,
        in_specs=(
            P("ctx", "head", None),
            P("ctx", None, None),
            P("ctx", None, None),
            P("ctx", "head", None),
            P(),
        ),
        out_specs=(P("ctx", "head", None), P("ctx", None, None), P("ctx", None, None)),
        check_vma=False,
    )
```
